32 devices in a mesh: level: 2 (over x), tile: 16 (over z, y, core).
Axes of the slice: x: 2, y: 2, z: 4, core: 2. Of those that a mesh axis runs over, the one named last changes fastest.
Arguments:
- density: float32 [2, 8, 8, 8, 2048], P('level', None, None, None, 'tile'), may hold values from 1 to 2
- momentum: float32 [2, 3, 8, 8, 8, 2048], P('level', None, None, None, None, 'tile'), may hold values from -0.3 to 0.3
- energy: float32 [2, 8, 8, 8, 2048], P('level', None, None, None, 'tile'), may hold values from 2.5 to 3.5
- rhs_older: float32 [2, 5, 8, 8, 8, 2048], P('level', None, None, None, None, 'tile'), may hold values from -4.5 to 4.5
- rhs_old: float32 [2, 5, 8, 8, 8, 2048], P('level', None, None, None, None, 'tile'), may hold values from -4.5 to 4.5
- peer_tile: int32 [16, 120], P('tile'), may hold values from 0 to 15, as said below
- peer_index: int32 [16, 120], P('tile'), may hold values from 0 to 119, as said below
- boundary_slot: int32 [16, 120], P('tile'), may hold values from 0 to 767, as said below
- face_partner: int32 [16, 768], P('tile'), may hold values from 0 to 767, as said below
- face_orient: int32 [16, 768], P('tile'), may hold values from 0 to 3, as said below
Outputs:
- tendency: float32 [2, 5, 8, 8, 8, 2048], P('level', None, None, None, None, 'tile')
The draws below stay inside these ranges and needn't reach their ends.
Inputs may be any that keep to these rules, and one draw needn't show every extreme that they name: `peer_tile`: never the tile itself; the partner's partner is the face itself; every two distinct tiles share exactly 8 face pairs. `peer_index`: consistent with peer_tile: the partner face's own entries point back to this face. `boundary_slot`: distinct within a tile, and these slots are exactly the slots that face_partner maps to themselves. `face_partner`: symmetric within a tile: slots not on the boundary come in pairs that name each other; boundary slots name themselves. `face_orient`: equal at both faces of every pair, within a tile and across tiles.
All inputs are finite; a program needn't handle non-finite values.
Results may differ from the reference program's by a relative error of at most 0.0001.
Values sent between devices are 32-bit elements; how exact they have to be, the bound alone decides.
A program may use at most 384 MiB of HBM per device.

```python
import jax
import jax.numpy as jnp
import numpy as np
from jax import lax

NP = 8
TSTEPS = 3
FCAP = 8
LEVELS = 2
TILES = 16
ELEMENTS = 2048
FACES = 768
FB = 120


def connectivity(key):
    base = jax.random.fold_in(key, 11)
    streams = jax.random.split(base, 7)
    rounds = FB // FCAP
    masks = jax.random.permutation(streams[0], TILES - 1)[:rounds] + 1
    position = jnp.arange(FB)
    round_of = position // FCAP
    mask_of = masks[round_of]
    relabel = jax.random.permutation(streams[2], TILES)
    restore = jnp.argsort(relabel)
    ordering = jax.vmap(lambda stream: jax.random.permutation(stream, FB))(jax.random.split(streams[3], TILES))
    unorder = jnp.argsort(ordering, axis=1)
    rows = jnp.arange(TILES)[:, None]
    other = jnp.bitwise_xor(rows, mask_of[unorder])
    tile_rel = relabel[other]
    index_rel = ordering[other, unorder]
    pair_table = jax.random.randint(streams[4], (TILES, FB), 0, 4)
    orient_rel = pair_table[jnp.minimum(rows, other), unorder]
    slot_perm = jax.vmap(lambda stream: jax.random.permutation(stream, FACES))(jax.random.split(streams[5], TILES))
    peer_tile = tile_rel[restore].astype(jnp.int32)
    peer_index = index_rel[restore].astype(jnp.int32)
    boundary_orient = orient_rel[restore].astype(jnp.int32)
    boundary_slot = slot_perm[:, :FB].astype(jnp.int32)
    left = slot_perm[:, FB::2]
    right = slot_perm[:, FB + 1::2]
    partner = jnp.broadcast_to(jnp.arange(FACES, dtype=jnp.int32), (TILES, FACES))
    partner = partner.at[rows, left].set(right.astype(jnp.int32)).at[rows, right].set(left.astype(jnp.int32))
    inner_orient = jax.random.randint(streams[6], (TILES, (FACES - FB) // 2), 0, 4).astype(jnp.int32)
    orient = jnp.zeros((TILES, FACES), jnp.int32)
    orient = orient.at[rows, left].set(inner_orient).at[rows, right].set(inner_orient)
    orient = orient.at[rows, boundary_slot].set(boundary_orient)
    return (peer_tile, peer_index, boundary_slot, partner, orient)


def draw_peer_tile(key, part):
    return connectivity(key)[0]


def draw_peer_index(key, part):
    return connectivity(key)[1]


def draw_boundary_slot(key, part):
    return connectivity(key)[2]


def draw_face_partner(key, part):
    return connectivity(key)[3]


def draw_face_orient(key, part):
    return connectivity(key)[4]


def level_of(own_key, extent, cuts, smallest, largest):
    gain = 1.0
    for axis_at, shards_of in cuts:
        steps = jax.random.uniform(jax.random.fold_in(jax.random.fold_in(own_key, 6), axis_at), (shards_of,), jnp.float32, smallest / len(cuts), largest / len(cuts))
        gain = gain * jnp.repeat(jnp.exp(steps), extent[axis_at] // shards_of).reshape((-1,) + (1,) * (len(extent) - 1 - axis_at))
    return gain


def gaussian(stream_key, dims, scale, reach, cuts=(), kind=jnp.bfloat16):
    array = jax.random.normal(stream_key, dims, jnp.float32) * scale
    if len(cuts) > 0:
        array = level_of(stream_key, dims, cuts, -0.22, 0.18) * array
    return jnp.clip(array, min=-reach, max=reach).astype(kind)


def setup_inputs(seed: int = 0) -> dict:
    arg_keys = jax.random.split(jax.random.key(seed), 11)
    return {
        "density": jnp.clip(1.0 + 1.0 * jax.random.uniform(arg_keys[0], (LEVELS, NP, NP, NP, ELEMENTS), jnp.float32) ** level_of(arg_keys[0], (LEVELS, NP, NP, NP, ELEMENTS), ((0, 2), (4, 16)), -0.2, 0.2), 1.0, 2.0),
        "momentum": jnp.clip(jax.random.uniform(arg_keys[1], (LEVELS, 3, NP, NP, NP, ELEMENTS), jnp.float32, -0.3, 0.3) * level_of(arg_keys[1], (LEVELS, 3, NP, NP, NP, ELEMENTS), ((0, 2), (5, 16)), -0.4, 0.0), -0.3, 0.3),
        "energy": jnp.clip(2.5 + 1.0 * jax.random.uniform(arg_keys[2], (LEVELS, NP, NP, NP, ELEMENTS), jnp.float32) ** level_of(arg_keys[2], (LEVELS, NP, NP, NP, ELEMENTS), ((0, 2), (4, 16)), -0.2, 0.2), 2.5, 3.5),
        "rhs_older": gaussian(arg_keys[3], (LEVELS, 5, NP, NP, NP, ELEMENTS), 1.5, 4.5, ((0, 2), (5, 16)), jnp.float32),
        "rhs_old": gaussian(arg_keys[4], (LEVELS, 5, NP, NP, NP, ELEMENTS), 1.5, 4.5, ((0, 2), (5, 16)), jnp.float32),
        "peer_tile": draw_peer_tile(jax.random.fold_in(arg_keys[10], 71), 0),
        "peer_index": draw_peer_index(jax.random.fold_in(arg_keys[10], 71), 0),
        "boundary_slot": draw_boundary_slot(jax.random.fold_in(arg_keys[10], 71), 0),
        "face_partner": draw_face_partner(jax.random.fold_in(arg_keys[10], 71), 0),
        "face_orient": draw_face_orient(jax.random.fold_in(arg_keys[10], 71), 0),
    }


step_size = 0.02
penalty = 2.5
metric = 0.1
lift_factor = 2.8
weight_back = -1.0 / 12.0
weight_here = 8.0 / 12.0
weight_next = 5.0 / 12.0


def lobatto_points():
    degree = NP - 1
    points = np.cos(np.pi * np.arange(degree + 1) / degree)
    table = np.zeros((degree + 1, degree + 1))
    for sweep in range(60):
        table[:, 0] = 1.0
        table[:, 1] = points
        for order in range(2, degree + 1):
            table[:, order] = ((2 * order - 1) * points * table[:, order - 1] - (order - 1) * table[:, order - 2]) / order
        points = points - (points * table[:, degree] - table[:, degree - 1]) / ((degree + 1) * table[:, degree])
    table[:, 0] = 1.0
    table[:, 1] = points
    for order in range(2, degree + 1):
        table[:, order] = ((2 * order - 1) * points * table[:, order - 1] - (order - 1) * table[:, order - 2]) / order
    return points[::-1], table[::-1, degree]


def derivative_table():
    degree = NP - 1
    points, values = lobatto_points()
    identity = np.eye(NP)
    spread = points[:, None] - points[None, :] + identity
    table = values[:, None] / values[None, :] / spread
    table = table * (1.0 - identity)
    table[0, 0] = -degree * (degree + 1) / 4.0
    table[degree, degree] = degree * (degree + 1) / 4.0
    return jnp.asarray(table, dtype=jnp.float32)


def directional_flux(state, direction):
    density_part = state[0]
    momenta = state[1:4]
    energy_part = state[4]
    velocity = momenta / density_part
    pressure = 0.4 * (energy_part - 0.5 * (momenta[0] * velocity[0] + momenta[1] * velocity[1] + momenta[2] * velocity[2]))
    carried = momenta[direction]
    pieces = [carried]
    for column in range(3):
        product = carried * velocity[column]
        if column == direction:
            product = product + pressure
        pieces.append(product)
    pieces.append((energy_part + pressure) * velocity[direction])
    return jnp.stack(pieces)


def face_traces(state, tiles):
    planes = []
    for which in range(6):
        direction = which // 2
        plane = jnp.take(state, (NP - 1) * (which % 2), axis=2 + direction)
        planes.append(plane.reshape(plane.shape[:4] + (tiles, plane.shape[4] // tiles)))
    stacked = jnp.stack(planes, axis=5)
    return stacked.reshape(stacked.shape[:4] + (-1,))


def oriented(raw, orient):
    turned = raw[:, :, ::-1, ::-1, :]
    first = jnp.where(orient >= 2, turned, raw)
    second = jnp.swapaxes(first, 2, 3)
    return jnp.where(orient % 2 == 1, second, first)


def tendency_of(state, partner_view, tiles):
    table = derivative_table()
    highest = lax.Precision.HIGHEST
    volume = jnp.einsum('ai,vbijke->vbajke', table, directional_flux(state, 0), precision=highest)
    volume = volume + jnp.einsum('aj,vbijke->vbiake', table, directional_flux(state, 1), precision=highest)
    volume = volume + jnp.einsum('ak,vbijke->vbijae', table, directional_flux(state, 2), precision=highest)
    result = -metric * volume
    traces = face_traces(state, tiles)
    view = partner_view(traces)
    grouped = traces.shape[:4] + (tiles, 6, -1)
    own_all = traces.reshape(grouped)
    far_all = view.reshape(grouped)
    for which in range(6):
        direction = which // 2
        normal = 2.0 * (which % 2) - 1.0
        own = own_all[:, :, :, :, :, which].reshape(traces.shape[:4] + (-1,))
        far = far_all[:, :, :, :, :, which].reshape(traces.shape[:4] + (-1,))
        jump = 0.5 * normal * (directional_flux(far, direction) - directional_flux(own, direction)) - 0.5 * penalty * (far - own)
        location = (slice(None),) * (2 + direction) + ((NP - 1) * (which % 2),)
        result = result.at[location].add(-lift_factor * jump)
    return result


def reference(density, momentum, energy, rhs_older, rhs_old, peer_tile, peer_index, boundary_slot, face_partner, face_orient):
    start = jnp.concatenate([density[:, None], momentum, energy[:, None]], axis=1)
    offsets = (jnp.arange(TILES, dtype=jnp.int32) * FACES)[:, None]
    inner_source = (offsets + face_partner).reshape(-1)
    target = (offsets + boundary_slot).reshape(-1)
    remote_slot = boundary_slot[peer_tile, peer_index]
    remote_source = (peer_tile * FACES + remote_slot).reshape(-1)
    gather_index = inner_source.at[target].set(remote_source)
    orient_flat = face_orient.reshape(-1)

    def partner_view(traces):
        return oriented(traces[..., gather_index], orient_flat)

    def level_rate(level_state):
        return tendency_of(level_state[:, None], partner_view, TILES)[:, 0]

    levels = jnp.arange(LEVELS, dtype=jnp.int32).reshape(-1, 1, 1, 1, 1, 1)
    state = start
    older = rhs_older
    old = rhs_old
    for repeat in range(TSTEPS):
        own_rate = lax.map(level_rate, state)
        below = jnp.concatenate([jnp.zeros_like(own_rate[:1]), own_rate[:-1]], axis=0)
        corrected = state + step_size * (own_rate - old) + step_size * (weight_back * older + weight_here * old + weight_next * below)
        predicted = state + step_size * own_rate
        state = jnp.where(levels == 0, predicted, corrected)
        older = old
        old = below
    return (state - start) / (TSTEPS * step_size)
```

```python
import jax
import jax.numpy as jnp
import numpy as np
from jax import lax
from jax.experimental import pallas as pl
from jax.experimental.pallas import tpu as pltpu
from jax.sharding import PartitionSpec as P

NP = 8
TSTEPS = 3
FCAP = 8


step_size = 0.02
penalty = 2.5
metric = 0.1
lift_factor = 2.8
weight_back = -1.0 / 12.0
weight_here = 8.0 / 12.0
weight_next = 5.0 / 12.0


def shifted(block, axis, distance):
    devices = range(lax.axis_size(axis))
    route = [(i - distance, i) for i in devices if i - distance in devices]
    return lax.ppermute(block, axis, route)


def lobatto_points():
    degree = NP - 1
    points = np.cos(np.pi * np.arange(degree + 1) / degree)
    table = np.zeros((degree + 1, degree + 1))
    for sweep in range(60):
        table[:, 0] = 1.0
        table[:, 1] = points
        for order in range(2, degree + 1):
            table[:, order] = (
                (2 * order - 1) * points * table[:, order - 1] - (order - 1) * table[:, order - 2]
            ) / order
        points = points - (points * table[:, degree] - table[:, degree - 1]) / (
            (degree + 1) * table[:, degree]
        )
    table[:, 0] = 1.0
    table[:, 1] = points
    for order in range(2, degree + 1):
        table[:, order] = (
            (2 * order - 1) * points * table[:, order - 1] - (order - 1) * table[:, order - 2]
        ) / order
    return (points[::-1], table[::-1, degree])


def derivative_numbers():
    degree = NP - 1
    points, values = lobatto_points()
    identity = np.eye(NP)
    spread = points[:, None] - points[None, :] + identity
    table = values[:, None] / values[None, :] / spread
    table = table * (1.0 - identity)
    table[0, 0] = -degree * (degree + 1) / 4.0
    table[degree, degree] = degree * (degree + 1) / 4.0
    return np.asarray(table, dtype=np.float32)

NV = 5
NODES = NP * NP
ROWS = NV * NODES


def primitive(w):
    inverse = 1.0 / w[0]
    velocity = [w[c] * inverse for c in (1, 2, 3)]
    pressure = 0.4 * (w[4] - 0.5 * (w[1] * velocity[0] + w[2] * velocity[1] + w[3] * velocity[2]))
    return velocity, pressure


def flux(w, velocity, pressure, direction):
    carried = w[1 + direction]
    parts = [carried]
    for column in range(3):
        product = carried * velocity[column]
        if column == direction:
            product = product + pressure
        parts.append(product)
    parts.append((w[4] + pressure) * velocity[direction])
    return parts


def pieces_of(x):
    high = x.astype(jnp.bfloat16)
    rest = x - high.astype(jnp.float32)
    middle = rest.astype(jnp.bfloat16)
    low = (rest - middle.astype(jnp.float32)).astype(jnp.bfloat16)
    return [high, middle, low]


def face_rows(which):
    direction, end = which // 2, (NP - 1) * (which % 2)
    return direction, end


def trace_rows(ref, which, v):
    direction, end = face_rows(which)
    base = v * NP * NODES
    if direction == 0:
        return ref[pl.ds(base + end * NODES, NODES), :]
    if direction == 1:
        return jnp.concatenate(
            [ref[pl.ds(base + i * NODES + end * NP, NP), :] for i in range(NP)], axis=0
        )
    return ref[pl.ds(base + end, NODES, stride=NP), :]


def trace_kernel(state, masks, turn, inner, send, raw, buffer, turned):
    width = state.shape[1]
    for which in range(6):
        lanes = pl.ds(which * width, width)
        mask = [jnp.broadcast_to(masks[o : o + 1, lanes], (NODES, width)) for o in range(4)]
        for v in range(NV):
            for at, piece in enumerate(pieces_of(trace_rows(state, which, v))):
                wide = piece.astype(jnp.float32)
                stacked = jnp.concatenate([(wide * m).astype(jnp.bfloat16) for m in mask], axis=0)
                out = jnp.dot(turn[...], stacked, preferred_element_type=jnp.float32)
                turned[at, pl.ds(v * NODES, NODES), lanes] = out.astype(jnp.bfloat16)
    total = None
    outgoing = None
    for at in range(3):
        block = turned[at]
        part = jnp.dot(block, inner[...], preferred_element_type=jnp.float32)
        leave = lax.dot_general(
            send[...], block, (((1,), (1,)), ((), ())), preferred_element_type=jnp.float32
        )
        total = part if total is None else total + part
        outgoing = leave if outgoing is None else outgoing + leave
    raw[...] = total
    buffer[...] = outgoing


def rate_kernel(state, raw, arrived, place, rolled, rate, view):
    width = state.shape[1]
    numbers = derivative_numbers()
    total = raw[...]
    for piece in pieces_of(arrived[...]):
        total = total + lax.dot_general(
            piece, place[...], (((0,), (0,)), ((), ())), preferred_element_type=jnp.float32
        )
    view[...] = total

    def combine(fields, target):
        result = None
        for index in range(NP):
            factor = float(-metric * numbers[target, index])
            if factor == 0.0:
                continue
            term = factor * fields[index]
            result = term if result is None else result + term
        return result

    def at(v, i, j):
        return pl.ds(pl.multiple_of(v * NP * NODES + i * NODES + j * NP, NP), NP)

    def along_first(j, carry):
        across = [[None] * NP for v in range(NV)]
        down = [[None] * NP for v in range(NV)]
        for i in range(NP):
            w = [state[at(v, i, j), :] for v in range(NV)]
            velocity, pressure = primitive(w)
            for v, part in enumerate(flux(w, velocity, pressure, 0)):
                across[v][i] = part
            for v, part in enumerate(flux(w, velocity, pressure, 2)):
                total = rolled[0] * part
                for shift in range(1, NP):
                    total = total + rolled[shift] * pltpu.roll(part, NP - shift, 0)
                down[v][i] = total
        for v in range(NV):
            for i in range(NP):
                rate[at(v, i, j), :] = combine(across[v], i) + down[v][i]
        return carry

    def along_second(i, carry):
        across = [[None] * NP for v in range(NV)]
        for j in range(NP):
            w = [state[at(v, i, j), :] for v in range(NV)]
            velocity, pressure = primitive(w)
            for v, part in enumerate(flux(w, velocity, pressure, 1)):
                across[v][j] = part
        for v in range(NV):
            for j in range(NP):
                rate[at(v, i, j), :] = rate[at(v, i, j), :] + combine(across[v], j)
        return carry

    lax.fori_loop(0, NP, along_first, 0)
    lax.fori_loop(0, NP, along_second, 0)

    for which in range(6):
        direction, end = face_rows(which)
        normal = 2.0 * (which % 2) - 1.0
        lanes = pl.ds(which * width, width)

        def lift(row, carry):
            def rows(v):
                base = v * NP * NODES
                if direction == 0:
                    return pl.ds(pl.multiple_of(base + end * NODES + row * NP, NP), NP)
                if direction == 1:
                    return pl.ds(pl.multiple_of(base + row * NODES + end * NP, NP), NP)
                return pl.ds(base + row * NODES + end, NP, stride=NP)

            own = [state[rows(v), :] for v in range(NV)]
            far = [
                view[pl.ds(pl.multiple_of(v * NODES + row * NP, NP), NP), lanes]
                for v in range(NV)
            ]
            own_flux = flux(own, *primitive(own), direction)
            far_flux = flux(far, *primitive(far), direction)
            for v in range(NV):
                jump = (0.5 * normal) * (far_flux[v] - own_flux[v]) - (0.5 * penalty) * (
                    far[v] - own[v]
                )
                rate[rows(v), :] = rate[rows(v), :] - lift_factor * jump
            return carry

        lax.fori_loop(0, NP, lift, 0)


VMEM = pl.BlockSpec(memory_space=pltpu.VMEM)


def traces_of(state, masks, turn, inner, send):
    slots = masks.shape[1]
    return pl.pallas_call(
        trace_kernel,
        out_shape=(
            jax.ShapeDtypeStruct((ROWS, slots), jnp.float32),
            jax.ShapeDtypeStruct((send.shape[0], ROWS), jnp.float32),
        ),
        in_specs=[VMEM] * 5,
        out_specs=(VMEM, VMEM),
        scratch_shapes=[pltpu.VMEM((3, ROWS, slots), jnp.bfloat16)],
        compiler_params=pltpu.CompilerParams(vmem_limit_bytes=40 << 20),
    )(state, masks, turn, inner, send)


def rate_of(state, raw, arrived, place, rolled):
    return pl.pallas_call(
        rate_kernel,
        out_shape=jax.ShapeDtypeStruct(state.shape, jnp.float32),
        in_specs=[VMEM] * 5,
        out_specs=VMEM,
        scratch_shapes=[pltpu.VMEM(raw.shape, jnp.float32)],
        compiler_params=pltpu.CompilerParams(vmem_limit_bytes=40 << 20),
    )(state, raw, arrived, place, rolled)


def turning():
    nodes = np.arange(NODES)
    blocks = []
    for orient in range(4):
        source = nodes.reshape(NP, NP)
        if orient >= 2:
            source = source[::-1, ::-1]
        if orient % 2 == 1:
            source = source.T
        block = np.zeros((NODES, NODES), np.float32)
        block[nodes, source.reshape(-1)] = 1.0
        blocks.append(block)
    return np.concatenate(blocks, axis=1)


def body(
    density,
    momentum,
    energy,
    rhs_older,
    rhs_old,
    peer_tile,
    peer_index,
    boundary_slot,
    face_partner,
    face_orient,
):
    width = density.shape[-1]
    start = jnp.concatenate(
        [
            density.reshape(-1, width),
            momentum.reshape(-1, width),
            energy.reshape(-1, width),
        ],
        axis=0,
    )
    level = lax.axis_index("level")
    levels = lax.axis_size("level")
    tiles = lax.axis_size("tile")
    peers = peer_tile[0]
    matches = peer_index[0]
    slots = boundary_slot[0]
    partner = face_partner[0]
    orient = face_orient[0]
    count = peers.shape[0]
    faces = partner.shape[0]
    same_peer = peers[:, None] == peers[None, :]
    listing = jnp.arange(count, dtype=jnp.int32)
    send_rank = jnp.sum(same_peer & (matches[None, :] < matches[:, None]), axis=1, dtype=jnp.int32)
    recv_rank = jnp.sum(same_peer & (listing[None, :] < listing[:, None]), axis=1, dtype=jnp.int32)
    places = jnp.arange(tiles * FCAP, dtype=jnp.int32)
    ids = jnp.arange(faces, dtype=jnp.int32)
    exact = jnp.bfloat16
    at_slot = (slots[:, None] == ids[None, :]).astype(exact)

    def routing(rank):
        onehot = (places[:, None] == (peers * FCAP + rank)[None, :]).astype(exact)
        return jnp.dot(onehot, at_slot, preferred_element_type=jnp.float32).astype(exact)

    send = routing(send_rank)
    place = routing(recv_rank)
    inner = ((ids[:, None] == partner[None, :]) & (partner != ids)[None, :]).astype(exact)
    masks = (orient[None, :] == jnp.arange(8, dtype=jnp.int32)[:, None]).astype(jnp.float32)
    turn = jnp.asarray(turning(), exact)
    numbers = derivative_numbers()
    diagonals = np.stack(
        [
            np.stack([-metric * numbers[k, (k + shift) % NP] for k in range(NP)])
            for shift in range(NP)
        ]
    ).astype(np.float32)
    rolled = jnp.broadcast_to(jnp.asarray(diagonals)[:, :, None], (NP, NP, width))

    def rates(states):
        traced = [traces_of(state, masks, turn, inner, send) for state in states]
        buffer = jnp.concatenate([leave for raw, leave in traced], axis=1)
        arrived = lax.all_to_all(buffer, "tile", split_axis=0, concat_axis=0, tiled=True)
        return [
            rate_of(state, raw, arrived[:, at * ROWS : (at + 1) * ROWS], place, rolled)
            for at, (state, (raw, leave)) in enumerate(zip(states, traced))
        ]

    older = rhs_older.reshape(-1, width)
    old = rhs_old.reshape(-1, width)

    def advance(state, own_rate, older, old, below):
        corrected = (
            state
            + step_size * (own_rate - old)
            + step_size * (weight_back * older + weight_here * old + weight_next * below)
        )
        return jnp.where(level == 0, state + step_size * own_rate, corrected)

    state = start
    if levels == 2:
        received = shifted(start, "level", 1)
        own_rate = rates([state])[0]
        received, own_rate = lax.optimization_barrier((received, own_rate))
        lower = jnp.where(level == 0, start, received)
        for repeat in range(TSTEPS):
            if repeat == 0:
                below = rates([lower])[0]
            else:
                own_rate, below = rates([state, lower])
            state = advance(state, own_rate, older, old, below)
            lower = lower + step_size * below
            older = old
            old = below
    else:
        for repeat in range(TSTEPS):
            own_rate = rates([state])[0]
            below = shifted(own_rate, "level", 1)
            state = advance(state, own_rate, older, old, below)
            older = old
            old = below
    return ((state - start) / (TSTEPS * step_size)).reshape(rhs_old.shape)


def solution(mesh):
    return jax.shard_map(
        body,
        mesh=mesh,
        in_specs=(
            P("level", None, None, None, "tile"),
            P("level", None, None, None, None, "tile"),
            P("level", None, None, None, "tile"),
            P("level", None, None, None, None, "tile"),
            P("level", None, None, None, None, "tile"),
            P("tile", None),
            P("tile", None),
            P("tile", None),
            P("tile", None),
            P("tile", None),
        ),
        out_specs=P("level", None, None, None, None, "tile"),
        check_vma=False,
    )
```

```python
import jax
import jax.numpy as jnp
import numpy as np
from jax import lax
from jax.experimental import pallas as pl
from jax.experimental.pallas import tpu as pltpu
from jax.sharding import PartitionSpec as P

NP = 8
TSTEPS = 3
FCAP = 8


step_size = 0.02
penalty = 2.5
metric = 0.1
lift_factor = 2.8
weight_back = -1.0 / 12.0
weight_here = 8.0 / 12.0
weight_next = 5.0 / 12.0


def shifted(block, axis, distance):
    devices = range(lax.axis_size(axis))
    route = [(i - distance, i) for i in devices if i - distance in devices]
    return lax.ppermute(block, axis, route)


def lobatto_points():
    degree = NP - 1
    points = np.cos(np.pi * np.arange(degree + 1) / degree)
    table = np.zeros((degree + 1, degree + 1))
    for sweep in range(60):
        table[:, 0] = 1.0
        table[:, 1] = points
        for order in range(2, degree + 1):
            table[:, order] = (
                (2 * order - 1) * points * table[:, order - 1] - (order - 1) * table[:, order - 2]
            ) / order
        points = points - (points * table[:, degree] - table[:, degree - 1]) / (
            (degree + 1) * table[:, degree]
        )
    table[:, 0] = 1.0
    table[:, 1] = points
    for order in range(2, degree + 1):
        table[:, order] = (
            (2 * order - 1) * points * table[:, order - 1] - (order - 1) * table[:, order - 2]
        ) / order
    return (points[::-1], table[::-1, degree])


def derivative_numbers():
    degree = NP - 1
    points, values = lobatto_points()
    identity = np.eye(NP)
    spread = points[:, None] - points[None, :] + identity
    table = values[:, None] / values[None, :] / spread
    table = table * (1.0 - identity)
    table[0, 0] = -degree * (degree + 1) / 4.0
    table[degree, degree] = degree * (degree + 1) / 4.0
    return np.asarray(table, dtype=np.float32)

NV = 5
NODES = NP * NP
ROWS = NV * NODES


def primitive(w):
    inverse = 1.0 / w[0]
    velocity = [w[c] * inverse for c in (1, 2, 3)]
    pressure = 0.4 * (w[4] - 0.5 * (w[1] * velocity[0] + w[2] * velocity[1] + w[3] * velocity[2]))
    return velocity, pressure


def flux(w, velocity, pressure, direction):
    carried = w[1 + direction]
    parts = [carried]
    for column in range(3):
        product = carried * velocity[column]
        if column == direction:
            product = product + pressure
        parts.append(product)
    parts.append((w[4] + pressure) * velocity[direction])
    return parts


def pieces_of(x):
    high = x.astype(jnp.bfloat16)
    rest = x - high.astype(jnp.float32)
    middle = rest.astype(jnp.bfloat16)
    low = (rest - middle.astype(jnp.float32)).astype(jnp.bfloat16)
    return [high, middle, low]


def face_rows(which):
    direction, end = which // 2, (NP - 1) * (which % 2)
    return direction, end


def trace_rows(ref, which, v):
    direction, end = face_rows(which)
    base = v * NP * NODES
    if direction == 0:
        return ref[pl.ds(base + end * NODES, NODES), :]
    if direction == 1:
        return jnp.concatenate(
            [ref[pl.ds(base + i * NODES + end * NP, NP), :] for i in range(NP)], axis=0
        )
    return ref[pl.ds(base + end, NODES, stride=NP), :]


def trace_kernel(state, masks, turn, inner, send, raw, buffer, turned):
    width = state.shape[1]
    for which in range(6):
        lanes = pl.ds(which * width, width)
        mask = [jnp.broadcast_to(masks[o : o + 1, lanes], (NODES, width)) for o in range(4)]
        for v in range(NV):
            for at, piece in enumerate(pieces_of(trace_rows(state, which, v))):
                wide = piece.astype(jnp.float32)
                stacked = jnp.concatenate([(wide * m).astype(jnp.bfloat16) for m in mask], axis=0)
                out = jnp.dot(turn[...], stacked, preferred_element_type=jnp.float32)
                turned[at, pl.ds(v * NODES, NODES), lanes] = out.astype(jnp.bfloat16)
    total = None
    outgoing = None
    for at in range(3):
        block = turned[at]
        part = jnp.dot(block, inner[...], preferred_element_type=jnp.float32)
        leave = lax.dot_general(
            send[...], block, (((1,), (1,)), ((), ())), preferred_element_type=jnp.float32
        )
        total = part if total is None else total + part
        outgoing = leave if outgoing is None else outgoing + leave
    raw[...] = total
    buffer[...] = outgoing


def rate_kernel(state, raw, arrived, place, rolled, rate, view):
    width = state.shape[1]
    numbers = derivative_numbers()
    total = raw[...]
    for piece in pieces_of(arrived[...]):
        total = total + lax.dot_general(
            piece, place[...], (((0,), (0,)), ((), ())), preferred_element_type=jnp.float32
        )
    view[...] = total

    def combine(fields, target):
        result = None
        for index in range(NP):
            factor = float(-metric * numbers[target, index])
            if factor == 0.0:
                continue
            term = factor * fields[index]
            result = term if result is None else result + term
        return result

    def at(v, i, j):
        return pl.ds(pl.multiple_of(v * NP * NODES + i * NODES + j * NP, NP), NP)

    def along_first(j, carry):
        across = [[None] * NP for v in range(NV)]
        down = [[None] * NP for v in range(NV)]
        for i in range(NP):
            w = [state[at(v, i, j), :] for v in range(NV)]
            velocity, pressure = primitive(w)
            for v, part in enumerate(flux(w, velocity, pressure, 0)):
                across[v][i] = part
            for v, part in enumerate(flux(w, velocity, pressure, 2)):
                total = rolled[0] * part
                for shift in range(1, NP):
                    total = total + rolled[shift] * pltpu.roll(part, NP - shift, 0)
                down[v][i] = total
        for v in range(NV):
            for i in range(NP):
                rate[at(v, i, j), :] = combine(across[v], i) + down[v][i]
        return carry

    def along_second(i, carry):
        across = [[None] * NP for v in range(NV)]
        for j in range(NP):
            w = [state[at(v, i, j), :] for v in range(NV)]
            velocity, pressure = primitive(w)
            for v, part in enumerate(flux(w, velocity, pressure, 1)):
                across[v][j] = part
        for v in range(NV):
            for j in range(NP):
                rate[at(v, i, j), :] = rate[at(v, i, j), :] + combine(across[v], j)
        return carry

    lax.fori_loop(0, NP, along_first, 0)
    lax.fori_loop(0, NP, along_second, 0)

    for which in range(6):
        direction, end = face_rows(which)
        normal = 2.0 * (which % 2) - 1.0
        lanes = pl.ds(which * width, width)

        def lift(row, carry):
            def rows(v):
                base = v * NP * NODES
                if direction == 0:
                    return pl.ds(pl.multiple_of(base + end * NODES + row * NP, NP), NP)
                if direction == 1:
                    return pl.ds(pl.multiple_of(base + row * NODES + end * NP, NP), NP)
                return pl.ds(base + row * NODES + end, NP, stride=NP)

            own = [state[rows(v), :] for v in range(NV)]
            far = [
                view[pl.ds(pl.multiple_of(v * NODES + row * NP, NP), NP), lanes]
                for v in range(NV)
            ]
            own_flux = flux(own, *primitive(own), direction)
            far_flux = flux(far, *primitive(far), direction)
            for v in range(NV):
                jump = (0.5 * normal) * (far_flux[v] - own_flux[v]) - (0.5 * penalty) * (
                    far[v] - own[v]
                )
                rate[rows(v), :] = rate[rows(v), :] - lift_factor * jump
            return carry

        lax.fori_loop(0, NP, lift, 0)


VMEM = pl.BlockSpec(memory_space=pltpu.VMEM)


def traces_of(state, masks, turn, inner, send):
    slots = masks.shape[1]
    return pl.pallas_call(
        trace_kernel,
        out_shape=(
            jax.ShapeDtypeStruct((ROWS, slots), jnp.float32),
            jax.ShapeDtypeStruct((send.shape[0], ROWS), jnp.float32),
        ),
        in_specs=[VMEM] * 5,
        out_specs=(VMEM, VMEM),
        scratch_shapes=[pltpu.VMEM((3, ROWS, slots), jnp.bfloat16)],
        compiler_params=pltpu.CompilerParams(vmem_limit_bytes=40 << 20),
    )(state, masks, turn, inner, send)


def rate_of(state, raw, arrived, place, rolled):
    return pl.pallas_call(
        rate_kernel,
        out_shape=jax.ShapeDtypeStruct(state.shape, jnp.float32),
        in_specs=[VMEM] * 5,
        out_specs=VMEM,
        scratch_shapes=[pltpu.VMEM(raw.shape, jnp.float32)],
        compiler_params=pltpu.CompilerParams(vmem_limit_bytes=40 << 20),
    )(state, raw, arrived, place, rolled)


def exchange_kernel(buffer, arrived, landed, send_sem, recv_sem):
    tiles = lax.axis_size("tile")
    me = lax.axis_index("tile")
    barrier = pltpu.get_barrier_semaphore()

    def peer(offset):
        return {"tile": lax.rem(me + offset, tiles)}

    def copy(offset):
        to = lax.rem(me + offset, tiles)
        return pltpu.make_async_remote_copy(
            src_ref=buffer.at[to],
            dst_ref=landed.at[me],
            send_sem=send_sem.at[offset],
            recv_sem=recv_sem.at[offset],
            device_id=peer(offset),
            device_id_type=pl.DeviceIdType.MESH,
        )

    def greet(offset, carry):
        pl.semaphore_signal(
            barrier, inc=1, device_id=peer(offset), device_id_type=pl.DeviceIdType.MESH
        )
        return carry

    def begin(offset, carry):
        copy(offset).start()
        return carry

    def finish(offset, carry):
        copy(offset).wait()
        return carry

    lax.fori_loop(1, tiles, greet, 0)
    pl.semaphore_wait(barrier, tiles - 1)
    lax.fori_loop(1, tiles, begin, 0)
    landed[me] = jnp.zeros(landed.shape[1:], jnp.float32)
    lax.fori_loop(1, tiles, finish, 0)
    arrived[...] = landed[...]


def exchanged(buffer, identifier):
    tiles = lax.axis_size("tile")
    blocks = buffer.reshape(tiles, -1, buffer.shape[1])
    return pl.pallas_call(
        exchange_kernel,
        out_shape=jax.ShapeDtypeStruct(blocks.shape, jnp.float32),
        in_specs=[VMEM],
        out_specs=VMEM,
        scratch_shapes=[
            pltpu.VMEM(blocks.shape, jnp.float32),
            pltpu.SemaphoreType.DMA((tiles,)),
            pltpu.SemaphoreType.DMA((tiles,)),
        ],
        compiler_params=pltpu.CompilerParams(
            collective_id=identifier, has_side_effects=True, vmem_limit_bytes=16 << 20
        ),
    )(blocks).reshape(buffer.shape)


def turning():
    nodes = np.arange(NODES)
    blocks = []
    for orient in range(4):
        source = nodes.reshape(NP, NP)
        if orient >= 2:
            source = source[::-1, ::-1]
        if orient % 2 == 1:
            source = source.T
        block = np.zeros((NODES, NODES), np.float32)
        block[nodes, source.reshape(-1)] = 1.0
        blocks.append(block)
    return np.concatenate(blocks, axis=1)


def body(
    density,
    momentum,
    energy,
    rhs_older,
    rhs_old,
    peer_tile,
    peer_index,
    boundary_slot,
    face_partner,
    face_orient,
):
    width = density.shape[-1]
    start = jnp.concatenate(
        [
            density.reshape(-1, width),
            momentum.reshape(-1, width),
            energy.reshape(-1, width),
        ],
        axis=0,
    )
    level = lax.axis_index("level")
    levels = lax.axis_size("level")
    tiles = lax.axis_size("tile")
    peers = peer_tile[0]
    matches = peer_index[0]
    slots = boundary_slot[0]
    partner = face_partner[0]
    orient = face_orient[0]
    count = peers.shape[0]
    faces = partner.shape[0]
    same_peer = peers[:, None] == peers[None, :]
    listing = jnp.arange(count, dtype=jnp.int32)
    send_rank = jnp.sum(same_peer & (matches[None, :] < matches[:, None]), axis=1, dtype=jnp.int32)
    recv_rank = jnp.sum(same_peer & (listing[None, :] < listing[:, None]), axis=1, dtype=jnp.int32)
    places = jnp.arange(tiles * FCAP, dtype=jnp.int32)
    ids = jnp.arange(faces, dtype=jnp.int32)
    exact = jnp.bfloat16
    at_slot = (slots[:, None] == ids[None, :]).astype(exact)

    def routing(rank):
        onehot = (places[:, None] == (peers * FCAP + rank)[None, :]).astype(exact)
        return jnp.dot(onehot, at_slot, preferred_element_type=jnp.float32).astype(exact)

    send = routing(send_rank)
    place = routing(recv_rank)
    inner = ((ids[:, None] == partner[None, :]) & (partner != ids)[None, :]).astype(exact)
    masks = (orient[None, :] == jnp.arange(8, dtype=jnp.int32)[:, None]).astype(jnp.float32)
    turn = jnp.asarray(turning(), exact)
    numbers = derivative_numbers()
    diagonals = np.stack(
        [
            np.stack([-metric * numbers[k, (k + shift) % NP] for k in range(NP)])
            for shift in range(NP)
        ]
    ).astype(np.float32)
    rolled = jnp.broadcast_to(jnp.asarray(diagonals)[:, :, None], (NP, NP, width))

    def rates(states):
        traced = [traces_of(state, masks, turn, inner, send) for state in states]
        buffer = jnp.concatenate([leave for raw, leave in traced], axis=1)
        arrived = exchanged(buffer, len(states) - 1)
        return [
            rate_of(state, raw, arrived[:, at * ROWS : (at + 1) * ROWS], place, rolled)
            for at, (state, (raw, leave)) in enumerate(zip(states, traced))
        ]

    older = rhs_older.reshape(-1, width)
    old = rhs_old.reshape(-1, width)

    def advance(state, own_rate, older, old, below):
        corrected = (
            state
            + step_size * (own_rate - old)
            + step_size * (weight_back * older + weight_here * old + weight_next * below)
        )
        return jnp.where(level == 0, state + step_size * own_rate, corrected)

    state = start
    if levels == 2:
        base = level == 0
        received = shifted(start, "level", 1)
        first = rates([start])[0]
        ahead = start + step_size * first
        second = rates([ahead])[0]
        third_state = ahead + step_size * second
        received, third_state = lax.optimization_barrier((received, third_state))
        lower = jnp.where(base, third_state, received)
        lower_first = rates([lower])[0]
        last_below = shifted(lower_first, "level", 1)
        state = advance(start, first, older, old, lower_first)
        lower = lower + step_size * lower_first
        own_second, lower_second = rates([state, lower])
        state = advance(state, own_second, old, lower_first, lower_second)
        own_third = rates([state])[0]
        own_third, last_below = lax.optimization_barrier((own_third, last_below))
        final = advance(state, own_third, lower_first, lower_second, last_below)
        state = jnp.where(base, third_state + step_size * lower_first, final)
    else:
        for repeat in range(TSTEPS):
            own_rate = rates([state])[0]
            below = shifted(own_rate, "level", 1)
            state = advance(state, own_rate, older, old, below)
            older = old
            old = below
    return ((state - start) / (TSTEPS * step_size)).reshape(rhs_old.shape)


def solution(mesh):
    return jax.shard_map(
        body,
        mesh=mesh,
        in_specs=(
            P("level", None, None, None, "tile"),
            P("level", None, None, None, None, "tile"),
            P("level", None, None, None, "tile"),
            P("level", None, None, None, None, "tile"),
            P("level", None, None, None, None, "tile"),
            P("tile", None),
            P("tile", None),
            P("tile", None),
            P("tile", None),
            P("tile", None),
        ),
        out_specs=P("level", None, None, None, None, "tile"),
        check_vma=False,
    )
```

```python
import functools

import jax
import jax.numpy as jnp
import numpy as np
from jax import lax
from jax.experimental import pallas as pl
from jax.experimental.pallas import tpu as pltpu
from jax.sharding import PartitionSpec as P

NP = 8
TSTEPS = 3
FCAP = 8


step_size = 0.02
penalty = 2.5
metric = 0.1
lift_factor = 2.8
weight_back = -1.0 / 12.0
weight_here = 8.0 / 12.0
weight_next = 5.0 / 12.0


def shifted(block, axis, distance):
    devices = range(lax.axis_size(axis))
    route = [(i - distance, i) for i in devices if i - distance in devices]
    return lax.ppermute(block, axis, route)


def lobatto_points():
    degree = NP - 1
    points = np.cos(np.pi * np.arange(degree + 1) / degree)
    table = np.zeros((degree + 1, degree + 1))
    for sweep in range(60):
        table[:, 0] = 1.0
        table[:, 1] = points
        for order in range(2, degree + 1):
            table[:, order] = (
                (2 * order - 1) * points * table[:, order - 1] - (order - 1) * table[:, order - 2]
            ) / order
        points = points - (points * table[:, degree] - table[:, degree - 1]) / (
            (degree + 1) * table[:, degree]
        )
    table[:, 0] = 1.0
    table[:, 1] = points
    for order in range(2, degree + 1):
        table[:, order] = (
            (2 * order - 1) * points * table[:, order - 1] - (order - 1) * table[:, order - 2]
        ) / order
    return (points[::-1], table[::-1, degree])


def derivative_numbers():
    degree = NP - 1
    points, values = lobatto_points()
    identity = np.eye(NP)
    spread = points[:, None] - points[None, :] + identity
    table = values[:, None] / values[None, :] / spread
    table = table * (1.0 - identity)
    table[0, 0] = -degree * (degree + 1) / 4.0
    table[degree, degree] = degree * (degree + 1) / 4.0
    return np.asarray(table, dtype=np.float32)

NV = 5
NODES = NP * NP
ROWS = NV * NODES


def primitive(w):
    inverse = 1.0 / w[0]
    velocity = [w[c] * inverse for c in (1, 2, 3)]
    pressure = 0.4 * (w[4] - 0.5 * (w[1] * velocity[0] + w[2] * velocity[1] + w[3] * velocity[2]))
    return velocity, pressure


def flux(w, velocity, pressure, direction):
    carried = w[1 + direction]
    parts = [carried]
    for column in range(3):
        product = carried * velocity[column]
        if column == direction:
            product = product + pressure
        parts.append(product)
    parts.append((w[4] + pressure) * velocity[direction])
    return parts


def pieces_of(x):
    high = x.astype(jnp.bfloat16)
    rest = x - high.astype(jnp.float32)
    middle = rest.astype(jnp.bfloat16)
    low = (rest - middle.astype(jnp.float32)).astype(jnp.bfloat16)
    return [high, middle, low]


def face_rows(which):
    direction, end = which // 2, (NP - 1) * (which % 2)
    return direction, end


def trace_rows(ref, which, v):
    direction, end = face_rows(which)
    base = v * NP * NODES
    if direction == 0:
        return ref[pl.ds(base + end * NODES, NODES), :]
    if direction == 1:
        return jnp.concatenate(
            [ref[pl.ds(base + i * NODES + end * NP, NP), :] for i in range(NP)], axis=0
        )
    return ref[pl.ds(base + end, NODES, stride=NP), :]


def gather_traces(state, masks, turn, turned):
    width = state.shape[1]
    for which in range(6):
        lanes = pl.ds(which * width, width)
        mask = [jnp.broadcast_to(masks[o : o + 1, lanes], (NODES, width)) for o in range(4)]
        for v in range(NV):
            for at, piece in enumerate(pieces_of(trace_rows(state, which, v))):
                wide = piece.astype(jnp.float32)
                stacked = jnp.concatenate([(wide * m).astype(jnp.bfloat16) for m in mask], axis=0)
                out = jnp.dot(turn[...], stacked, preferred_element_type=jnp.float32)
                turned[at, pl.ds(v * NODES, NODES), lanes] = out.astype(jnp.bfloat16)


def outgoing_of(turned, send):
    outgoing = None
    for at in range(3):
        leave = lax.dot_general(
            send[...], turned[at], (((1,), (1,)), ((), ())), preferred_element_type=jnp.float32
        )
        outgoing = leave if outgoing is None else outgoing + leave
    return outgoing


def inner_of(turned, inner):
    total = None
    for at in range(3):
        part = jnp.dot(turned[at], inner[...], preferred_element_type=jnp.float32)
        total = part if total is None else total + part
    return total


def outer_of(arrived, place):
    total = None
    for piece in pieces_of(arrived):
        part = lax.dot_general(
            piece, place[...], (((0,), (0,)), ((), ())), preferred_element_type=jnp.float32
        )
        total = part if total is None else total + part
    return total


def volume_of(state, rolled, rate):
    numbers = derivative_numbers()

    def combine(fields, target):
        result = None
        for index in range(NP):
            factor = float(-metric * numbers[target, index])
            if factor == 0.0:
                continue
            term = factor * fields[index]
            result = term if result is None else result + term
        return result

    def at(v, i, j):
        return pl.ds(pl.multiple_of(v * NP * NODES + i * NODES + j * NP, NP), NP)

    def along_first(j, carry):
        across = [[None] * NP for v in range(NV)]
        down = [[None] * NP for v in range(NV)]
        for i in range(NP):
            w = [state[at(v, i, j), :] for v in range(NV)]
            velocity, pressure = primitive(w)
            for v, part in enumerate(flux(w, velocity, pressure, 0)):
                across[v][i] = part
            for v, part in enumerate(flux(w, velocity, pressure, 2)):
                total = rolled[0] * part
                for shift in range(1, NP):
                    total = total + rolled[shift] * pltpu.roll(part, NP - shift, 0)
                down[v][i] = total
        for v in range(NV):
            for i in range(NP):
                rate[at(v, i, j), :] = combine(across[v], i) + down[v][i]
        return carry

    def along_second(i, carry):
        across = [[None] * NP for v in range(NV)]
        for j in range(NP):
            w = [state[at(v, i, j), :] for v in range(NV)]
            velocity, pressure = primitive(w)
            for v, part in enumerate(flux(w, velocity, pressure, 1)):
                across[v][j] = part
        for v in range(NV):
            for j in range(NP):
                rate[at(v, i, j), :] = rate[at(v, i, j), :] + combine(across[v], j)
        return carry

    lax.fori_loop(0, NP, along_first, 0)
    lax.fori_loop(0, NP, along_second, 0)


def lift_faces(state, view, rate):
    width = state.shape[1]
    for which in range(6):
        direction, end = face_rows(which)
        normal = 2.0 * (which % 2) - 1.0
        lanes = pl.ds(which * width, width)

        def lift(row, carry):
            def rows(v):
                base = v * NP * NODES
                if direction == 0:
                    return pl.ds(pl.multiple_of(base + end * NODES + row * NP, NP), NP)
                if direction == 1:
                    return pl.ds(pl.multiple_of(base + row * NODES + end * NP, NP), NP)
                return pl.ds(base + row * NODES + end, NP, stride=NP)

            own = [state[rows(v), :] for v in range(NV)]
            far = [
                view[pl.ds(pl.multiple_of(v * NODES + row * NP, NP), NP), lanes]
                for v in range(NV)
            ]
            own_flux = flux(own, *primitive(own), direction)
            far_flux = flux(far, *primitive(far), direction)
            for v in range(NV):
                jump = (0.5 * normal) * (far_flux[v] - own_flux[v]) - (0.5 * penalty) * (
                    far[v] - own[v]
                )
                rate[rows(v), :] = rate[rows(v), :] - lift_factor * jump
            return carry

        lax.fori_loop(0, NP, lift, 0)


VMEM = pl.BlockSpec(memory_space=pltpu.VMEM)


def rate_kernel(count, *refs):
    states, refs = refs[:count], refs[count:]
    masks, turn, inner, send, place, rolled = refs[:6]
    rates, refs = refs[6 : 6 + count], refs[6 + count :]
    turned, views, buffer, landed, send_sem, recv_sem = refs
    tiles = lax.axis_size("tile")
    me = lax.axis_index("tile")
    barrier = pltpu.get_barrier_semaphore()

    def peer(offset):
        return {"tile": lax.rem(me + offset, tiles)}

    def copy(offset):
        return pltpu.make_async_remote_copy(
            src_ref=buffer.at[lax.rem(me + offset, tiles)],
            dst_ref=landed.at[me],
            send_sem=send_sem.at[offset],
            recv_sem=recv_sem.at[offset],
            device_id=peer(offset),
            device_id_type=pl.DeviceIdType.MESH,
        )

    def greet(offset, carry):
        pl.semaphore_signal(
            barrier, inc=1, device_id=peer(offset), device_id_type=pl.DeviceIdType.MESH
        )
        return carry

    def begin(offset, carry):
        copy(offset).start()
        return carry

    def finish(offset, carry):
        copy(offset).wait()
        return carry

    lax.fori_loop(1, tiles, greet, 0)
    for at in range(count):
        gather_traces(states[at], masks, turn, turned.at[at])
        leave = outgoing_of(turned.at[at], send)
        buffer[:, at * FCAP : (at + 1) * FCAP, :] = leave.reshape(tiles, FCAP, ROWS)
    pl.semaphore_wait(barrier, tiles - 1)
    lax.fori_loop(1, tiles, begin, 0)
    landed[me] = jnp.zeros(landed.shape[1:], jnp.float32)
    for at in range(count):
        views[at] = inner_of(turned.at[at], inner)
        volume_of(states[at], rolled, rates[at])
    lax.fori_loop(1, tiles, finish, 0)
    for at in range(count):
        arrived = landed[:, at * FCAP : (at + 1) * FCAP, :].reshape(tiles * FCAP, ROWS)
        views[at] = views[at] + outer_of(arrived, place)
        lift_faces(states[at], views.at[at], rates[at])


def rates_of(states, tables):
    tiles = lax.axis_size("tile")
    count = len(states)
    slots = tables[0].shape[1]
    like = jax.ShapeDtypeStruct(states[0].shape, jnp.float32)
    return pl.pallas_call(
        functools.partial(rate_kernel, count),
        out_shape=[like] * count,
        in_specs=[VMEM] * (count + len(tables)),
        out_specs=[VMEM] * count,
        scratch_shapes=[
            pltpu.VMEM((count, 3, ROWS, slots), jnp.bfloat16),
            pltpu.VMEM((count, ROWS, slots), jnp.float32),
            pltpu.VMEM((tiles, count * FCAP, ROWS), jnp.float32),
            pltpu.VMEM((tiles, count * FCAP, ROWS), jnp.float32),
            pltpu.SemaphoreType.DMA((tiles,)),
            pltpu.SemaphoreType.DMA((tiles,)),
        ],
        compiler_params=pltpu.CompilerParams(
            collective_id=count - 1, has_side_effects=True, vmem_limit_bytes=40 << 20
        ),
    )(*states, *tables)


def turning():
    nodes = np.arange(NODES)
    blocks = []
    for orient in range(4):
        source = nodes.reshape(NP, NP)
        if orient >= 2:
            source = source[::-1, ::-1]
        if orient % 2 == 1:
            source = source.T
        block = np.zeros((NODES, NODES), np.float32)
        block[nodes, source.reshape(-1)] = 1.0
        blocks.append(block)
    return np.concatenate(blocks, axis=1)


def body(
    density,
    momentum,
    energy,
    rhs_older,
    rhs_old,
    peer_tile,
    peer_index,
    boundary_slot,
    face_partner,
    face_orient,
):
    width = density.shape[-1]
    start = jnp.concatenate(
        [
            density.reshape(-1, width),
            momentum.reshape(-1, width),
            energy.reshape(-1, width),
        ],
        axis=0,
    )
    level = lax.axis_index("level")
    levels = lax.axis_size("level")
    tiles = lax.axis_size("tile")
    peers = peer_tile[0]
    matches = peer_index[0]
    slots = boundary_slot[0]
    partner = face_partner[0]
    orient = face_orient[0]
    count = peers.shape[0]
    faces = partner.shape[0]
    same_peer = peers[:, None] == peers[None, :]
    listing = jnp.arange(count, dtype=jnp.int32)
    send_rank = jnp.sum(same_peer & (matches[None, :] < matches[:, None]), axis=1, dtype=jnp.int32)
    recv_rank = jnp.sum(same_peer & (listing[None, :] < listing[:, None]), axis=1, dtype=jnp.int32)
    places = jnp.arange(tiles * FCAP, dtype=jnp.int32)
    ids = jnp.arange(faces, dtype=jnp.int32)
    exact = jnp.bfloat16
    at_slot = (slots[:, None] == ids[None, :]).astype(exact)

    def routing(rank):
        onehot = (places[:, None] == (peers * FCAP + rank)[None, :]).astype(exact)
        return jnp.dot(onehot, at_slot, preferred_element_type=jnp.float32).astype(exact)

    send = routing(send_rank)
    place = routing(recv_rank)
    inner = ((ids[:, None] == partner[None, :]) & (partner != ids)[None, :]).astype(exact)
    masks = (orient[None, :] == jnp.arange(8, dtype=jnp.int32)[:, None]).astype(jnp.float32)
    turn = jnp.asarray(turning(), exact)
    numbers = derivative_numbers()
    diagonals = np.stack(
        [
            np.stack([-metric * numbers[k, (k + shift) % NP] for k in range(NP)])
            for shift in range(NP)
        ]
    ).astype(np.float32)
    rolled = jnp.broadcast_to(jnp.asarray(diagonals)[:, :, None], (NP, NP, width))

    tables = (masks, turn, inner, send, place, rolled)

    def rates(states):
        return rates_of(states, tables)

    older = rhs_older.reshape(-1, width)
    old = rhs_old.reshape(-1, width)

    def advance(state, own_rate, older, old, below):
        corrected = (
            state
            + step_size * (own_rate - old)
            + step_size * (weight_back * older + weight_here * old + weight_next * below)
        )
        return jnp.where(level == 0, state + step_size * own_rate, corrected)

    state = start
    if levels == 2:
        base = level == 0
        received = shifted(start, "level", 1)
        first = rates([start])[0]
        ahead = start + step_size * first
        second = rates([ahead])[0]
        third_state = ahead + step_size * second
        received, third_state = lax.optimization_barrier((received, third_state))
        lower = jnp.where(base, third_state, received)
        lower_first = rates([lower])[0]
        last_below = shifted(lower_first, "level", 1)
        state = advance(start, first, older, old, lower_first)
        lower = lower + step_size * lower_first
        own_second, lower_second = rates([state, lower])
        state = advance(state, own_second, old, lower_first, lower_second)
        own_third = rates([state])[0]
        own_third, last_below = lax.optimization_barrier((own_third, last_below))
        final = advance(state, own_third, lower_first, lower_second, last_below)
        state = jnp.where(base, third_state + step_size * lower_first, final)
    else:
        for repeat in range(TSTEPS):
            own_rate = rates([state])[0]
            below = shifted(own_rate, "level", 1)
            state = advance(state, own_rate, older, old, below)
            older = old
            old = below
    return ((state - start) / (TSTEPS * step_size)).reshape(rhs_old.shape)


def solution(mesh):
    return jax.shard_map(
        body,
        mesh=mesh,
        in_specs=(
            P("level", None, None, None, "tile"),
            P("level", None, None, None, None, "tile"),
            P("level", None, None, None, "tile"),
            P("level", None, None, None, None, "tile"),
            P("level", None, None, None, None, "tile"),
            P("tile", None),
            P("tile", None),
            P("tile", None),
            P("tile", None),
            P("tile", None),
        ),
        out_specs=P("level", None, None, None, None, "tile"),
        check_vma=False,
    )
```

```python
import functools

import jax
import jax.numpy as jnp
import numpy as np
from jax import lax
from jax.experimental import pallas as pl
from jax.experimental.pallas import tpu as pltpu
from jax.sharding import PartitionSpec as P

NP = 8
TSTEPS = 3
FCAP = 8


step_size = 0.02
penalty = 2.5
metric = 0.1
lift_factor = 2.8
weight_back = -1.0 / 12.0
weight_here = 8.0 / 12.0
weight_next = 5.0 / 12.0


def shifted(block, axis, distance):
    devices = range(lax.axis_size(axis))
    route = [(i - distance, i) for i in devices if i - distance in devices]
    return lax.ppermute(block, axis, route)


def lobatto_points():
    degree = NP - 1
    points = np.cos(np.pi * np.arange(degree + 1) / degree)
    table = np.zeros((degree + 1, degree + 1))
    for sweep in range(60):
        table[:, 0] = 1.0
        table[:, 1] = points
        for order in range(2, degree + 1):
            table[:, order] = (
                (2 * order - 1) * points * table[:, order - 1] - (order - 1) * table[:, order - 2]
            ) / order
        points = points - (points * table[:, degree] - table[:, degree - 1]) / (
            (degree + 1) * table[:, degree]
        )
    table[:, 0] = 1.0
    table[:, 1] = points
    for order in range(2, degree + 1):
        table[:, order] = (
            (2 * order - 1) * points * table[:, order - 1] - (order - 1) * table[:, order - 2]
        ) / order
    return (points[::-1], table[::-1, degree])


def derivative_numbers():
    degree = NP - 1
    points, values = lobatto_points()
    identity = np.eye(NP)
    spread = points[:, None] - points[None, :] + identity
    table = values[:, None] / values[None, :] / spread
    table = table * (1.0 - identity)
    table[0, 0] = -degree * (degree + 1) / 4.0
    table[degree, degree] = degree * (degree + 1) / 4.0
    return np.asarray(table, dtype=np.float32)

NV = 5
NODES = NP * NP
ROWS = NV * NODES


def primitive(w):
    inverse = 1.0 / w[0]
    velocity = [w[c] * inverse for c in (1, 2, 3)]
    pressure = 0.4 * (w[4] - 0.5 * (w[1] * velocity[0] + w[2] * velocity[1] + w[3] * velocity[2]))
    return velocity, pressure


def flux(w, velocity, pressure, direction):
    carried = w[1 + direction]
    parts = [carried]
    for column in range(3):
        product = carried * velocity[column]
        if column == direction:
            product = product + pressure
        parts.append(product)
    parts.append((w[4] + pressure) * velocity[direction])
    return parts


def pieces_of(x):
    high = x.astype(jnp.bfloat16)
    rest = x - high.astype(jnp.float32)
    middle = rest.astype(jnp.bfloat16)
    low = (rest - middle.astype(jnp.float32)).astype(jnp.bfloat16)
    return [high, middle, low]


def face_rows(which):
    direction, end = which // 2, (NP - 1) * (which % 2)
    return direction, end


def trace_rows(ref, which, v):
    direction, end = face_rows(which)
    base = v * NP * NODES
    if direction == 0:
        return ref[pl.ds(base + end * NODES, NODES), :]
    if direction == 1:
        return jnp.concatenate(
            [ref[pl.ds(base + i * NODES + end * NP, NP), :] for i in range(NP)], axis=0
        )
    return ref[pl.ds(base + end, NODES, stride=NP), :]


def gather_traces(state, masks, turn, turned):
    width = state.shape[1]
    for which in range(6):
        lanes = pl.ds(which * width, width)
        mask = [jnp.broadcast_to(masks[o : o + 1, lanes], (NODES, width)) for o in range(4)]
        for v in range(NV):
            for at, piece in enumerate(pieces_of(trace_rows(state, which, v))):
                wide = piece.astype(jnp.float32)
                stacked = jnp.concatenate([(wide * m).astype(jnp.bfloat16) for m in mask], axis=0)
                out = jnp.dot(turn[...], stacked, preferred_element_type=jnp.float32)
                turned[at, pl.ds(v * NODES, NODES), lanes] = out.astype(jnp.bfloat16)


def outgoing_of(turned, send):
    outgoing = None
    for at in range(3):
        leave = lax.dot_general(
            send[...], turned[at], (((1,), (1,)), ((), ())), preferred_element_type=jnp.float32
        )
        outgoing = leave if outgoing is None else outgoing + leave
    return outgoing


def inner_of(turned, inner):
    total = None
    for at in range(3):
        part = jnp.dot(turned[at], inner[...], preferred_element_type=jnp.float32)
        total = part if total is None else total + part
    return total


def outer_of(arrived, place):
    total = None
    for piece in pieces_of(arrived):
        part = lax.dot_general(
            piece, place[...], (((0,), (0,)), ((), ())), preferred_element_type=jnp.float32
        )
        total = part if total is None else total + part
    return total


def volume_of(state, rolled, rate):
    numbers = derivative_numbers()

    def derived(fields):
        even = [fields[index] + fields[NP - 1 - index] for index in range(NP // 2)]
        odd = [fields[index] - fields[NP - 1 - index] for index in range(NP // 2)]
        results = [None] * NP
        for target in range(NP // 2):
            near = None
            far = None
            for index in range(NP // 2):
                here = float(numbers[target, index])
                there = float(numbers[target, NP - 1 - index])
                one = (-0.5 * metric * (here + there)) * even[index]
                two = (-0.5 * metric * (here - there)) * odd[index]
                near = one if near is None else near + one
                far = two if far is None else far + two
            results[target] = far + near
            results[NP - 1 - target] = far - near
        return results

    def at(v, i, j):
        return pl.ds(pl.multiple_of(v * NP * NODES + i * NODES + j * NP, NP), NP)

    def along_first(j, carry):
        across = [[None] * NP for v in range(NV)]
        down = [[None] * NP for v in range(NV)]
        for i in range(NP):
            w = [state[at(v, i, j), :] for v in range(NV)]
            velocity, pressure = primitive(w)
            for v, part in enumerate(flux(w, velocity, pressure, 0)):
                across[v][i] = part
            for v, part in enumerate(flux(w, velocity, pressure, 2)):
                total = rolled[0] * part
                for shift in range(1, NP):
                    total = total + rolled[shift] * pltpu.roll(part, NP - shift, 0)
                down[v][i] = total
        for v in range(NV):
            for i, part in enumerate(derived(across[v])):
                rate[at(v, i, j), :] = part + down[v][i]
        return carry

    def along_second(i, carry):
        across = [[None] * NP for v in range(NV)]
        for j in range(NP):
            w = [state[at(v, i, j), :] for v in range(NV)]
            velocity, pressure = primitive(w)
            for v, part in enumerate(flux(w, velocity, pressure, 1)):
                across[v][j] = part
        for v in range(NV):
            for j, part in enumerate(derived(across[v])):
                rate[at(v, i, j), :] = rate[at(v, i, j), :] + part
        return carry

    lax.fori_loop(0, NP, along_first, 0)
    lax.fori_loop(0, NP, along_second, 0)


def lift_faces(state, view, rate):
    width = state.shape[1]
    for which in range(6):
        direction, end = face_rows(which)
        normal = 2.0 * (which % 2) - 1.0
        lanes = pl.ds(which * width, width)

        def lift(row, carry):
            def rows(v):
                base = v * NP * NODES
                if direction == 0:
                    return pl.ds(pl.multiple_of(base + end * NODES + row * NP, NP), NP)
                if direction == 1:
                    return pl.ds(pl.multiple_of(base + row * NODES + end * NP, NP), NP)
                return pl.ds(base + row * NODES + end, NP, stride=NP)

            own = [state[rows(v), :] for v in range(NV)]
            far = [
                view[pl.ds(pl.multiple_of(v * NODES + row * NP, NP), NP), lanes]
                for v in range(NV)
            ]
            own_flux = flux(own, *primitive(own), direction)
            far_flux = flux(far, *primitive(far), direction)
            for v in range(NV):
                jump = (0.5 * normal) * (far_flux[v] - own_flux[v]) - (0.5 * penalty) * (
                    far[v] - own[v]
                )
                rate[rows(v), :] = rate[rows(v), :] - lift_factor * jump
            return carry

        lax.fori_loop(0, NP, lift, 0)


VMEM = pl.BlockSpec(memory_space=pltpu.VMEM)


def rate_kernel(count, *refs):
    states, refs = refs[:count], refs[count:]
    masks, turn, inner, send, place, rolled = refs[:6]
    rates, refs = refs[6 : 6 + count], refs[6 + count :]
    turned, views, buffer, landed, send_sem, recv_sem = refs
    tiles = lax.axis_size("tile")
    me = lax.axis_index("tile")
    barrier = pltpu.get_barrier_semaphore()

    def peer(offset):
        return {"tile": lax.rem(me + offset, tiles)}

    def copy(offset):
        return pltpu.make_async_remote_copy(
            src_ref=buffer.at[lax.rem(me + offset, tiles)],
            dst_ref=landed.at[me],
            send_sem=send_sem.at[offset],
            recv_sem=recv_sem.at[offset],
            device_id=peer(offset),
            device_id_type=pl.DeviceIdType.MESH,
        )

    def greet(offset, carry):
        pl.semaphore_signal(
            barrier, inc=1, device_id=peer(offset), device_id_type=pl.DeviceIdType.MESH
        )
        return carry

    def begin(offset, carry):
        copy(offset).start()
        return carry

    def finish(offset, carry):
        copy(offset).wait()
        return carry

    lax.fori_loop(1, tiles, greet, 0)
    for at in range(count):
        gather_traces(states[at], masks, turn, turned.at[at])
        leave = outgoing_of(turned.at[at], send)
        buffer[:, at * FCAP : (at + 1) * FCAP, :] = leave.reshape(tiles, FCAP, ROWS)
    pl.semaphore_wait(barrier, tiles - 1)
    lax.fori_loop(1, tiles, begin, 0)
    landed[me] = jnp.zeros(landed.shape[1:], jnp.float32)
    for at in range(count):
        views[at] = inner_of(turned.at[at], inner)
        volume_of(states[at], rolled, rates[at])
    lax.fori_loop(1, tiles, finish, 0)
    for at in range(count):
        arrived = landed[:, at * FCAP : (at + 1) * FCAP, :].reshape(tiles * FCAP, ROWS)
        views[at] = views[at] + outer_of(arrived, place)
        lift_faces(states[at], views.at[at], rates[at])


def rates_of(states, tables):
    tiles = lax.axis_size("tile")
    count = len(states)
    slots = tables[0].shape[1]
    like = jax.ShapeDtypeStruct(states[0].shape, jnp.float32)
    return pl.pallas_call(
        functools.partial(rate_kernel, count),
        out_shape=[like] * count,
        in_specs=[VMEM] * (count + len(tables)),
        out_specs=[VMEM] * count,
        scratch_shapes=[
            pltpu.VMEM((count, 3, ROWS, slots), jnp.bfloat16),
            pltpu.VMEM((count, ROWS, slots), jnp.float32),
            pltpu.VMEM((tiles, count * FCAP, ROWS), jnp.float32),
            pltpu.VMEM((tiles, count * FCAP, ROWS), jnp.float32),
            pltpu.SemaphoreType.DMA((tiles,)),
            pltpu.SemaphoreType.DMA((tiles,)),
        ],
        compiler_params=pltpu.CompilerParams(
            collective_id=count - 1, has_side_effects=True, vmem_limit_bytes=40 << 20
        ),
    )(*states, *tables)


def turning():
    nodes = np.arange(NODES)
    blocks = []
    for orient in range(4):
        source = nodes.reshape(NP, NP)
        if orient >= 2:
            source = source[::-1, ::-1]
        if orient % 2 == 1:
            source = source.T
        block = np.zeros((NODES, NODES), np.float32)
        block[nodes, source.reshape(-1)] = 1.0
        blocks.append(block)
    return np.concatenate(blocks, axis=1)


def body(
    density,
    momentum,
    energy,
    rhs_older,
    rhs_old,
    peer_tile,
    peer_index,
    boundary_slot,
    face_partner,
    face_orient,
):
    width = density.shape[-1]
    start = jnp.concatenate(
        [
            density.reshape(-1, width),
            momentum.reshape(-1, width),
            energy.reshape(-1, width),
        ],
        axis=0,
    )
    level = lax.axis_index("level")
    levels = lax.axis_size("level")
    tiles = lax.axis_size("tile")
    peers = peer_tile[0]
    matches = peer_index[0]
    slots = boundary_slot[0]
    partner = face_partner[0]
    orient = face_orient[0]
    count = peers.shape[0]
    faces = partner.shape[0]
    same_peer = peers[:, None] == peers[None, :]
    listing = jnp.arange(count, dtype=jnp.int32)
    send_rank = jnp.sum(same_peer & (matches[None, :] < matches[:, None]), axis=1, dtype=jnp.int32)
    recv_rank = jnp.sum(same_peer & (listing[None, :] < listing[:, None]), axis=1, dtype=jnp.int32)
    places = jnp.arange(tiles * FCAP, dtype=jnp.int32)
    ids = jnp.arange(faces, dtype=jnp.int32)
    exact = jnp.bfloat16
    at_slot = (slots[:, None] == ids[None, :]).astype(exact)

    def routing(rank):
        onehot = (places[:, None] == (peers * FCAP + rank)[None, :]).astype(exact)
        return jnp.dot(onehot, at_slot, preferred_element_type=jnp.float32).astype(exact)

    send = routing(send_rank)
    place = routing(recv_rank)
    inner = ((ids[:, None] == partner[None, :]) & (partner != ids)[None, :]).astype(exact)
    masks = (orient[None, :] == jnp.arange(8, dtype=jnp.int32)[:, None]).astype(jnp.float32)
    turn = jnp.asarray(turning(), exact)
    numbers = derivative_numbers()
    diagonals = np.stack(
        [
            np.stack([-metric * numbers[k, (k + shift) % NP] for k in range(NP)])
            for shift in range(NP)
        ]
    ).astype(np.float32)
    rolled = jnp.broadcast_to(jnp.asarray(diagonals)[:, :, None], (NP, NP, width))

    tables = (masks, turn, inner, send, place, rolled)

    def rates(states):
        return rates_of(states, tables)

    older = rhs_older.reshape(-1, width)
    old = rhs_old.reshape(-1, width)

    def advance(state, own_rate, older, old, below):
        corrected = (
            state
            + step_size * (own_rate - old)
            + step_size * (weight_back * older + weight_here * old + weight_next * below)
        )
        return jnp.where(level == 0, state + step_size * own_rate, corrected)

    state = start
    if levels == 2:
        base = level == 0
        received = shifted(start, "level", 1)
        first = rates([start])[0]
        ahead = start + step_size * first
        second = rates([ahead])[0]
        third_state = ahead + step_size * second
        received, third_state = lax.optimization_barrier((received, third_state))
        lower = jnp.where(base, third_state, received)
        lower_first = rates([lower])[0]
        last_below = shifted(lower_first, "level", 1)
        state = advance(start, first, older, old, lower_first)
        lower = lower + step_size * lower_first
        own_second, lower_second = rates([state, lower])
        state = advance(state, own_second, old, lower_first, lower_second)
        own_third = rates([state])[0]
        own_third, last_below = lax.optimization_barrier((own_third, last_below))
        final = advance(state, own_third, lower_first, lower_second, last_below)
        state = jnp.where(base, third_state + step_size * lower_first, final)
    else:
        for repeat in range(TSTEPS):
            own_rate = rates([state])[0]
            below = shifted(own_rate, "level", 1)
            state = advance(state, own_rate, older, old, below)
            older = old
            old = below
    return ((state - start) / (TSTEPS * step_size)).reshape(rhs_old.shape)


def solution(mesh):
    return jax.shard_map(
        body,
        mesh=mesh,
        in_specs=(
            P("level", None, None, None, "tile"),
            P("level", None, None, None, None, "tile"),
            P("level", None, None, None, "tile"),
            P("level", None, None, None, None, "tile"),
            P("level", None, None, None, None, "tile"),
            P("tile", None),
            P("tile", None),
            P("tile", None),
            P("tile", None),
            P("tile", None),
        ),
        out_specs=P("level", None, None, None, None, "tile"),
        check_vma=False,
    )
```
